256 devices in a mesh: basis: 32 (over z_lo, y, core), state: 8 (over x, z_hi).
Axes of the slice: x: 4, y: 4, z: 8 (z_hi: 2, z_lo: 4; z = z_hi * 4 + z_lo), core: 2. Of those that a mesh axis runs over, the one named last changes fastest.
Arguments:
- vectors: bfloat16 [512, 163840], P('state', 'basis'), may hold values from -6 to 6
- blocks: bfloat16 [1280, 72, 128, 128], P('basis', 'state'), may hold values from -0.0625 to 0.0625
- columns: int32 [1280, 72], P('basis', 'state'), may hold values from 0 to 1279, as said below
- counts: int32 [1280], P('basis'), may hold values from 18 to 72, as said below
Outputs:
- sigma: bfloat16 [512, 163840], P('state', 'basis')
The draws below stay inside these ranges and needn't reach their ends.
Inputs may be any that keep to these rules, and one draw needn't show every extreme that they name: Every block column lies within 36 blocks of its block row and inside the basis; a row's slots name distinct columns except near the basis ends, where a column may repeat. Slots k < counts[r] are live; some block row has all 72 slots live.
All inputs are finite; a program needn't handle non-finite values.
Results may differ from the reference program's by a relative error of at most 0.001.
Values may be sent and summed in bfloat16 or wider, within the bound.
A program may use at most 192 MiB of HBM per device.

```python
import jax
import jax.numpy as jnp
from jax import lax

B = 128
S = 512
W = 36
NB = 1280
N = 163840
K = 72


def draw_columns(key, part):
    row_keys = jax.random.split(jax.random.fold_in(key, 11), NB)
    offsets = jax.vmap(lambda single: jax.random.permutation(single, 2 * W + 1))(row_keys)[:, :K] - W
    row_index = jnp.arange(NB, dtype=jnp.int32)[:, None]
    target = row_index + offsets.astype(jnp.int32)
    target = jnp.where(target < 0, -target, target)
    target = jnp.where(target > NB - 1, 2 * (NB - 1) - target, target)
    return target.astype(jnp.int32)


def draw_counts(key, part):
    first_key, second_key = jax.random.split(jax.random.fold_in(key, 23))
    values = jax.random.randint(first_key, (NB,), max(1, K // 4), K + 1, dtype=jnp.int32)
    where_full = jax.random.randint(second_key, (), 0, NB, dtype=jnp.int32)
    return values.at[where_full].set(K).astype(jnp.int32)


def level_of(stream_key, extent, cuts, smallest, top_value):
    factor_of, own = 1.0, jax.random.fold_in(stream_key, 6)
    for position, blocks in cuts:
        draws = jnp.exp(jax.random.uniform(jax.random.fold_in(own, position), (blocks,), jnp.float32, smallest / len(cuts), top_value / len(cuts)))
        factor_of = factor_of * jnp.repeat(draws, extent[position] // blocks).reshape([-1 if axis == position else 1 for axis in range(len(extent))])
    return factor_of


def normal_values(stream_key, shape, width, bound, cuts=(), held_as=jnp.bfloat16):
    level = level_of(stream_key, shape, cuts, -0.22, 0.18) if cuts else 1.0
    array = jax.random.normal(stream_key, shape, jnp.float32) * width * level
    return jnp.minimum(jnp.maximum(array, -bound), bound).astype(held_as)


def setup_inputs(seed: int = 0) -> dict:
    key_of = jax.random.split(jax.random.key(seed), 5)
    return {
        "vectors": normal_values(key_of[0], (S, N), 1.0, 6.0, ((0, 8), (1, 32))),
        "blocks": normal_values(key_of[1], (NB, K, B, B), (B * K) ** -0.5, 0.0625, ((0, 32), (1, 8))),
        "columns": draw_columns(jax.random.fold_in(key_of[4], 71), 0),
        "counts": draw_counts(jax.random.fold_in(key_of[4], 71), 0),
    }


def reference(vectors, blocks, columns, counts):
    vector_blocks = vectors.reshape(S, NB, B)

    def one_row(pieces):
        panel, column_list, live_count = pieces
        picked = jnp.take(vector_blocks, column_list, axis=1).astype(jnp.float32)
        live_mask = (jnp.arange(K) < live_count).astype(jnp.float32)
        picked = picked * live_mask[None, :, None]
        return jnp.einsum("skb,kcb->sc", picked, panel.astype(jnp.float32))

    result = lax.map(one_row, (blocks, columns, counts))
    return jnp.transpose(result, (1, 0, 2)).reshape(S, NB * B).astype(jnp.bfloat16)
```

```python
import functools

import jax
import jax.numpy as jnp
from jax import lax
from jax.experimental import pallas as pl
from jax.experimental.pallas import tpu as pltpu
from jax.sharding import PartitionSpec as P

W = 36
X, Z_HI, Z_LO = 4, 2, 4
STEP_ROWS = 4


def x_perm(shift):
    return [(x * Z_HI + h, (x + shift) % X * Z_HI + h) for x in range(X) for h in range(Z_HI)]


def z_perm(shift, basis, state):
    inner = basis // Z_LO
    pairs = []
    for b in range(basis):
        z_lo, rest = divmod(b, inner)
        for s in range(state):
            x, z_hi = divmod(s, Z_HI)
            z = (z_hi * Z_LO + z_lo + shift) % (Z_HI * Z_LO)
            target = (z % Z_LO * inner + rest) * state + x * Z_HI + z // Z_LO
            pairs.append((b * state + s, target))
    return pairs


def from_x(value, shift):
    return lax.ppermute(value, "state", x_perm(-shift))


def across_z(value, step):
    pairs = z_perm(step, lax.axis_size("basis"), lax.axis_size("state"))
    return lax.ppermute(lax.ppermute(value, ("basis", "state"), pairs), ("basis", "state"), pairs)


def product_kernel(spans, slots, relative, live, blocks, *refs):
    pieces, outs, (panel, sems) = refs[:12], refs[12:16], refs[16:]
    states, size = outs[0].shape[0], blocks.shape[2]

    @pl.when(pl.program_id(0) == 0)
    def _():
        copies = []
        for i, piece in enumerate(pieces):
            source, width, target = spans[i % 3]
            copies.append(
                pltpu.make_async_copy(
                    piece.at[:, pl.ds(source, width)],
                    panel.at[pl.ds(i // 3 * states, states), pl.ds(target, width)],
                    sems.at[i],
                )
            )
        for copy in copies:
            copy.start()
        for copy in copies:
            copy.wait()

    for row in range(STEP_ROWS):
        base = (pl.program_id(0) * STEP_ROWS + row) * slots
        total = None
        for first in range(0, slots, 2):
            group = range(first, min(first + 2, slots))
            picked = [
                panel[:, pl.ds(pl.multiple_of(relative[base + k] * size, size), size)] for k in group
            ]
            weight = [
                jnp.where(live[base + k] > 0, blocks[row, k], jnp.zeros_like(blocks[row, k]))
                for k in group
            ]
            term = lax.dot_general(
                jnp.concatenate(picked, axis=1),
                jnp.concatenate(weight, axis=1),
                (((1,), (1,)), ((), ())),
                preferred_element_type=jnp.float32,
            )
            total = term if total is None else total + term
        for i, out in enumerate(outs):
            out[:, row * size : (row + 1) * size] = total[i * states : (i + 1) * states]


def product(half, relative, live, blocks, pieces):
    rows, slots, size, _ = blocks.shape
    part = rows // 2
    states = pieces[0].shape[0]
    lead = W - half * part if half else W
    tail = W if half else W - (rows - part)
    spans = (
        ((rows - lead) * size, lead * size, 0),
        (0, rows * size, lead * size),
        (0, tail * size, (lead + rows) * size),
    )
    steps = part // STEP_ROWS
    width = (part + 2 * W) * size
    grid_spec = pltpu.PrefetchScalarGridSpec(
        num_scalar_prefetch=2,
        grid=(steps,),
        in_specs=[
            pl.BlockSpec(
                (STEP_ROWS, slots, size, size), lambda i, *_: (half * steps + i, 0, 0, 0)
            )
        ]
        + [pl.BlockSpec(memory_space=pl.ANY)] * 12,
        out_specs=[pl.BlockSpec((states, STEP_ROWS * size), lambda i, *_: (0, i))] * 4,
        scratch_shapes=[
            pltpu.VMEM((4 * states, width), jnp.bfloat16),
            pltpu.SemaphoreType.DMA((12,)),
        ],
    )
    return pl.pallas_call(
        functools.partial(product_kernel, spans, slots),
        grid_spec=grid_spec,
        out_shape=[jax.ShapeDtypeStruct((states, part * size), jnp.float32)] * 4,
        compiler_params=pltpu.CompilerParams(vmem_limit_bytes=40 * 1024 * 1024),
        cost_estimate=pl.CostEstimate(
            flops=2 * part * slots * size * size * 4 * states * 3,
            bytes_accessed=4 * states * width * 2 + part * slots * size * size * 2,
            transcendentals=0,
        ),
    )(relative, live, blocks, *pieces)


def with_neighbours(piece):
    size = lax.axis_size("basis")
    up = [(i, i + 1) for i in range(size - 1)]
    down = [(j, i) for i, j in up]
    return (lax.ppermute(piece, "basis", up), piece, lax.ppermute(piece, "basis", down))


def on_device(vectors, blocks, columns, counts):
    rows, slots, size, _ = blocks.shape
    part = rows // 2
    first_block = lax.axis_index("basis") * rows - W
    relative = columns - first_block
    slot_index = lax.axis_index("state") * slots + jnp.arange(slots, dtype=jnp.int32)
    live = (slot_index[None, :] < counts[:, None]).astype(jnp.int32)

    cut = vectors.shape[0] // 2
    other = jnp.concatenate(
        [across_z(vectors[:cut], 2), across_z(vectors[cut:], -2)], axis=0
    )
    sums = []
    for mine, forward in ((other, -1), (vectors, 1)):
        right, left = from_x(mine, 1), from_x(mine, -1)
        opposite = from_x(right if forward == 1 else left, forward)
        pieces = [p for piece in (mine, right, left, opposite) for p in with_neighbours(piece)]
        partial = [
            product(
                h,
                (relative[h * part : (h + 1) * part] - h * part).reshape(-1),
                live[h * part : (h + 1) * part].reshape(-1),
                blocks,
                pieces,
            )
            for h in range(2)
        ]
        (own_a, right_a, left_a, far_a), (own_b, right_b, left_b, far_b) = partial
        total_a = own_a + from_x(right_a + from_x(far_a, -1), -1) + from_x(left_a, 1)
        total_b = own_b + from_x(right_b, -1) + from_x(left_b + from_x(far_b, 1), 1)
        sums.append((total_a, total_b))
    (away_a, away_b), (kept_a, kept_b) = sums
    sigma = jnp.concatenate(
        [kept_a + across_z(away_a, 2), kept_b + across_z(away_b, -2)], axis=1
    )
    return sigma.astype(jnp.bfloat16)


def solution(mesh):
    in_specs = (
        P("state", "basis"),
        P("basis", "state", None, None),
        P("basis", "state"),
        P("basis"),
    )
    out_specs = P("state", "basis")
    return jax.shard_map(
        on_device, mesh=mesh, in_specs=in_specs, out_specs=out_specs, check_vma=False
    )
```

```python
import functools

import jax
import jax.numpy as jnp
from jax import lax
from jax.experimental import pallas as pl
from jax.experimental.pallas import tpu as pltpu
from jax.sharding import PartitionSpec as P

W = 36
X, Z_HI, Z_LO = 4, 2, 4
STEP_ROWS = 4
CHUNKS = 4
MESH = pl.DeviceIdType.MESH


def places():
    basis, state = lax.axis_index("basis"), lax.axis_index("state")
    inner = lax.axis_size("basis") // Z_LO
    x, z_hi = lax.div(state, Z_HI), lax.rem(state, Z_HI)
    z_lo, rest = lax.div(basis, inner), lax.rem(basis, inner)
    z = z_hi * Z_LO + z_lo

    def along_x(shift):
        return (basis, lax.rem(x + shift + X, X) * Z_HI + z_hi)

    def along_z(shift):
        moved = lax.rem(z + shift + Z_HI * Z_LO, Z_HI * Z_LO)
        return (lax.rem(moved, Z_LO) * inner + rest, x * Z_HI + lax.div(moved, Z_LO))

    return {
        "right": along_x(1),
        "left": along_x(-1),
        "ahead": along_z(2),
        "behind": along_z(-2),
    }


def greet(partners):
    barrier = pltpu.get_barrier_semaphore()
    for device in partners:
        pl.semaphore_signal(barrier, inc=1, device_id=device, device_id_type=MESH)
    pl.semaphore_wait(barrier, len(partners))


def sender(send_sems, recv_sems):
    used = iter(range(send_sems.shape[0]))

    def make(source, target, device):
        n = next(used)
        return pltpu.make_async_remote_copy(
            src_ref=source,
            dst_ref=target,
            send_sem=send_sems.at[n],
            recv_sem=recv_sems.at[n],
            device_id=device,
            device_id_type=MESH,
        )

    return make


def gather_kernel(vectors, mine, low, high, relay, send_sems, recv_sems):
    at = places()
    basis, state = lax.axis_index("basis"), lax.axis_index("state")
    devices = lax.axis_size("basis")
    up = (lax.rem(basis + 1, devices), state)
    down = (lax.rem(basis + devices - 1, devices), state)
    has_up, has_down = basis < devices - 1, basis > 0
    make = sender(send_sems, recv_sems)
    width, reach = vectors.shape[1], low.shape[2]
    cut = vectors.shape[0] // 2
    halves = (pl.ds(0, cut), pl.ds(cut, cut))

    greet([*at.values(), up, down])

    plain, edges = [], []

    def start(copy):
        copy.start()
        plain.append(copy)
        return copy

    def halo(piece, source):
        rising = make(source.at[:, pl.ds(width - reach, reach)], low.at[piece], up)
        falling = make(source.at[:, pl.ds(0, reach)], high.at[piece], down)

        @pl.when(has_up)
        def _():
            rising.start()

        @pl.when(has_down)
        def _():
            falling.start()

        edges.append((rising, falling))

    z_routes = ("ahead", "behind")
    first = [
        start(make(vectors.at[half], relay.at[half], at[route]))
        for half, route in zip(halves, z_routes)
    ]

    def spread(base, source):
        to_left = start(make(source, mine.at[base], at["left"]))
        to_right = start(make(source, mine.at[base + 1], at["right"]))
        halo(base, source)
        return to_left, to_right

    def forward(base, to_left, to_right):
        to_left.wait_recv()
        far = [start(make(mine.at[base, halves[0]], mine.at[base + 2, halves[0]], at["left"]))]
        halo(base + 1, mine.at[base])
        to_right.wait_recv()
        far.append(
            start(make(mine.at[base + 1, halves[1]], mine.at[base + 2, halves[1]], at["right"]))
        )
        halo(base + 2, mine.at[base + 1])
        return far

    own = spread(0, vectors)
    second = []
    for copy, half, route in zip(first, halves, z_routes):
        copy.wait_recv()
        second.append(start(make(relay.at[half], mine.at[3, half], at[route])))
    own_far = forward(0, *own)
    for copy in second:
        copy.wait_recv()
    other = spread(4, mine.at[3])
    for copy in own_far:
        copy.wait_recv()
    halo(3, mine.at[2])
    other_far = forward(4, *other)
    for copy in other_far:
        copy.wait_recv()
    halo(7, mine.at[6])

    for copy in plain:
        copy.wait_send()
    for rising, falling in edges:

        @pl.when(has_up)
        def _():
            rising.wait_send()
            falling.wait_recv()

        @pl.when(has_down)
        def _():
            falling.wait_send()
            rising.wait_recv()


def gather(vectors, size):
    states, width = vectors.shape
    reach = W * size
    copies = 2 + 2 + 2 * 4 + 8 * 2
    anywhere = pl.BlockSpec(memory_space=pl.ANY)
    return pl.pallas_call(
        gather_kernel,
        out_shape=[
            jax.ShapeDtypeStruct((7, states, width), vectors.dtype),
            jax.ShapeDtypeStruct((8, states, reach), vectors.dtype),
            jax.ShapeDtypeStruct((8, states, reach), vectors.dtype),
            jax.ShapeDtypeStruct((states, width), vectors.dtype),
        ],
        in_specs=[anywhere],
        out_specs=[anywhere] * 4,
        scratch_shapes=[
            pltpu.SemaphoreType.DMA((copies,)),
            pltpu.SemaphoreType.DMA((copies,)),
        ],
        compiler_params=pltpu.CompilerParams(collective_id=0, has_side_effects=True),
    )(vectors)[:3]


def product_kernel(slots, relative, live, blocks, vectors, mine, low, high, out, panel, sems):
    states, size = out.shape[1], blocks.shape[2]
    width, reach = vectors.shape[1], low.shape[2]

    @pl.when(pl.program_id(0) == 0)
    def _():
        copies = []
        for piece in range(8):
            rows = pl.ds(piece * states, states)
            middle = vectors if piece == 0 else mine.at[piece - 1]
            for source, start, length in (
                (low.at[piece], 0, reach),
                (middle, reach, width),
                (high.at[piece], reach + width, reach),
            ):
                copies.append(
                    pltpu.make_async_copy(
                        source, panel.at[rows, pl.ds(start, length)], sems.at[len(copies)]
                    )
                )
        for copy in copies:
            copy.start()
        for copy in copies:
            copy.wait()

    for row in range(STEP_ROWS):
        base = (pl.program_id(0) * STEP_ROWS + row) * slots
        total = None
        for first in range(0, slots, 2):
            group = range(first, min(first + 2, slots))
            picked = [
                panel[:, pl.ds(pl.multiple_of(relative[base + k] * size, size), size)] for k in group
            ]
            weight = [
                jnp.where(live[base + k] > 0, blocks[row, k], jnp.zeros_like(blocks[row, k]))
                for k in group
            ]
            term = lax.dot_general(
                jnp.concatenate(picked, axis=1),
                jnp.concatenate(weight, axis=1),
                (((1,), (1,)), ((), ())),
                preferred_element_type=jnp.float32,
            )
            total = term if total is None else total + term
        out[:, :, row * size : (row + 1) * size] = total.reshape(8, states, size)


def product(relative, live, blocks, vectors, mine, low, high):
    rows, slots, size, _ = blocks.shape
    states, width = vectors.shape
    anywhere = pl.BlockSpec(memory_space=pl.ANY)
    grid_spec = pltpu.PrefetchScalarGridSpec(
        num_scalar_prefetch=2,
        grid=(rows // STEP_ROWS,),
        in_specs=[
            pl.BlockSpec((STEP_ROWS, slots, size, size), lambda i, *_: (i, 0, 0, 0)),
        ]
        + [anywhere] * 4,
        out_specs=pl.BlockSpec((8, states, STEP_ROWS * size), lambda i, *_: (0, 0, i)),
        scratch_shapes=[
            pltpu.VMEM((8 * states, width + 2 * W * size), jnp.bfloat16),
            pltpu.SemaphoreType.DMA((24,)),
        ],
    )
    return pl.pallas_call(
        functools.partial(product_kernel, slots),
        grid_spec=grid_spec,
        out_shape=jax.ShapeDtypeStruct((8, states, width), jnp.float32),
        compiler_params=pltpu.CompilerParams(vmem_limit_bytes=40 * 1024 * 1024),
    )(relative, live, blocks, vectors, mine, low, high)


def reduce_kernel(partial, out, passing, joined, direct, relay, away, send_sems, recv_sems):
    at = places()
    greet(list(at.values()))
    make = sender(send_sems, recv_sems)
    chunk = partial.shape[2] // CHUNKS
    started = []

    def start(source, target, device):
        copy = make(source, target, device)
        copy.start()
        started.append(copy)
        return copy

    def part(z, piece, q):
        return partial.at[z * 4 + piece, :, pl.ds(q * chunk, chunk)]

    units = [(z, q) for z in (1, 0) for q in range(CHUNKS)]
    index = {unit: n for n, unit in enumerate(units)}
    ways = (("right", "left", 1, 2), ("left", "right", 2, 1))
    far, near, joint, hop, final = {}, {}, {}, {}, {}

    def send(unit):
        z, q = unit
        to, back, _, plain = ways[q % 2]
        n = index[unit]
        far[unit] = start(part(z, 3, q), passing.at[n], at[to])
        near[unit] = start(part(z, plain, q), direct.at[n], at[back])

    def join(unit):
        z, q = unit
        to, _, piece, _ = ways[q % 2]
        n = index[unit]
        far[unit].wait_recv()
        passing[n] = part(z, piece, q)[...] + passing[n]
        joint[unit] = start(passing.at[n], joined.at[n], at[to])

    def finish(unit):
        z, q = unit
        n = index[unit]
        joint[unit].wait_recv()
        near[unit].wait_recv()
        joined[n] = part(z, 0, q)[...] + joined[n] + direct[n]
        if z == 1:
            route = at["ahead" if q % 2 == 0 else "behind"]
            hop[q] = start(joined.at[n], relay.at[q], route)

    def pass_on(q):
        hop[q].wait_recv()
        route = at["ahead" if q % 2 == 0 else "behind"]
        final[q] = start(relay.at[q], away.at[q], route)

    pairs = [units[i : i + 2] for i in range(0, len(units), 2)]
    half = CHUNKS // 2
    for unit in pairs[0]:
        send(unit)
    for n, pair in enumerate(pairs):
        if n + 1 < len(pairs):
            for unit in pairs[n + 1]:
                send(unit)
        for unit in pair:
            join(unit)
        if n >= 1:
            for unit in pairs[n - 1]:
                finish(unit)
        if 2 <= n < 2 + half:
            for unit in pairs[n - 2]:
                pass_on(unit[1])
    for unit in pairs[-1]:
        finish(unit)
    for q in range(CHUNKS):
        if q not in final:
            pass_on(q)
    for q in range(CHUNKS):
        final[q].wait_recv()
        columns = pl.ds(q * chunk, chunk)
        out[:, columns] = (joined[index[(0, q)]] + away[q]).astype(out.dtype)
    for copy in started:
        copy.wait_send()


def reduce(partial):
    _, states, width = partial.shape
    chunk = width // CHUNKS
    copies = 2 * CHUNKS * 3 + CHUNKS * 2
    in_vmem = pl.BlockSpec(memory_space=pltpu.VMEM)
    slots = pltpu.VMEM((2 * CHUNKS, states, chunk), jnp.float32)
    return pl.pallas_call(
        reduce_kernel,
        out_shape=jax.ShapeDtypeStruct((states, width), jnp.bfloat16),
        in_specs=[in_vmem],
        out_specs=in_vmem,
        scratch_shapes=[
            slots,
            slots,
            slots,
            pltpu.VMEM((CHUNKS, states, chunk), jnp.float32),
            pltpu.VMEM((CHUNKS, states, chunk), jnp.float32),
            pltpu.SemaphoreType.DMA((copies,)),
            pltpu.SemaphoreType.DMA((copies,)),
        ],
        compiler_params=pltpu.CompilerParams(
            collective_id=1, has_side_effects=True, vmem_limit_bytes=40 * 1024 * 1024
        ),
    )(partial)


def on_device(vectors, blocks, columns, counts):
    rows, slots, size, _ = blocks.shape
    first_block = lax.axis_index("basis") * rows - W
    relative = (columns - first_block).reshape(-1)
    slot_index = lax.axis_index("state") * slots + jnp.arange(slots, dtype=jnp.int32)
    live = (slot_index[None, :] < counts[:, None]).astype(jnp.int32).reshape(-1)
    mine, low, high = gather(vectors, size)
    return reduce(product(relative, live, blocks, vectors, mine, low, high))


def solution(mesh):
    in_specs = (
        P("state", "basis"),
        P("basis", "state", None, None),
        P("basis", "state"),
        P("basis"),
    )
    out_specs = P("state", "basis")
    return jax.shard_map(
        on_device, mesh=mesh, in_specs=in_specs, out_specs=out_specs, check_vma=False
    )
```

```python
import jax
import jax.numpy as jnp
from jax import lax
from jax.experimental import pallas as pl
from jax.experimental.pallas import tpu as pltpu
from jax.sharding import PartitionSpec as P

W = 36
X, Z_HI, Z_LO = 4, 2, 4
CHUNKS = 4
MESH = pl.DeviceIdType.MESH


def places():
    basis, state = lax.axis_index("basis"), lax.axis_index("state")
    inner = lax.axis_size("basis") // Z_LO
    x, z_hi = lax.div(state, Z_HI), lax.rem(state, Z_HI)
    z_lo, rest = lax.div(basis, inner), lax.rem(basis, inner)
    z = z_hi * Z_LO + z_lo

    def along_x(shift):
        return (basis, lax.rem(x + shift + X, X) * Z_HI + z_hi)

    def along_z(shift):
        moved = lax.rem(z + shift + Z_HI * Z_LO, Z_HI * Z_LO)
        return (lax.rem(moved, Z_LO) * inner + rest, x * Z_HI + lax.div(moved, Z_LO))

    return {
        "right": along_x(1),
        "left": along_x(-1),
        "ahead": along_z(2),
        "behind": along_z(-2),
    }


def greet(partners):
    barrier = pltpu.get_barrier_semaphore()
    for device in partners:
        pl.semaphore_signal(barrier, inc=1, device_id=device, device_id_type=MESH)
    pl.semaphore_wait(barrier, len(partners))


def sender(send_sems, recv_sems):
    used = iter(range(send_sems.shape[0]))

    def make(source, target, device):
        n = next(used)
        return pltpu.make_async_remote_copy(
            src_ref=source,
            dst_ref=target,
            send_sem=send_sems.at[n],
            recv_sem=recv_sems.at[n],
            device_id=device,
            device_id_type=MESH,
        )

    return make


def sigma_kernel(
    relative, live, vectors, blocks, out,
    own_panel, other_panel, held, relay, partial, passing, joined, direct, hopping, away,
    send_sems, recv_sems, local_sems,
):
    at = places()
    basis, state = lax.axis_index("basis"), lax.axis_index("state")
    devices = lax.axis_size("basis")
    up = (lax.rem(basis + 1, devices), state)
    down = (lax.rem(basis + devices - 1, devices), state)
    has_up, has_down = basis < devices - 1, basis > 0
    make = sender(send_sems, recv_sems)
    states = vectors.shape[1]
    rows, slots, size, _ = blocks.shape
    width = rows * size
    cut = states // 2
    halves = (pl.ds(0, cut), pl.ds(cut, cut))
    panels = (own_panel, other_panel)
    z_routes = ("ahead", "behind")

    greet([*at.values(), up, down])
    started, edges = [], {}

    def start(source, target, device):
        copy = make(source, target, device)
        copy.start()
        started.append(copy)
        return copy

    def middle(z, piece, first=0, count=states):
        return panels[z].at[pl.ds(W, rows), pl.ds(piece * states + first, count)]

    def halo(z, piece, source):
        lines = pl.ds(piece * states, states)
        low = panels[z].at[pl.ds(0, W), lines]
        high = panels[z].at[pl.ds(W + rows, W), lines]
        rising = make(source.at[pl.ds(rows - W, W)], low, up)
        falling = make(source.at[pl.ds(0, W)], high, down)

        @pl.when(has_up)
        def _():
            rising.start()

        @pl.when(has_down)
        def _():
            falling.start()

        edges[z, piece] = (rising, falling)

    def spread(z, source):
        to_left = start(source, middle(z, 1), at["left"])
        to_right = start(source, middle(z, 2), at["right"])
        halo(z, 0, source)
        return to_left, to_right

    def forward(z, to_left, to_right):
        to_left.wait_recv()
        far = [start(middle(z, 1, 0, cut), middle(z, 3, 0, cut), at["left"])]
        halo(z, 1, middle(z, 1))
        to_right.wait_recv()
        far.append(start(middle(z, 2, cut, cut), middle(z, 3, cut, cut), at["right"]))
        halo(z, 2, middle(z, 2))
        return far

    def edges_arrived(z):
        for piece in range(4):
            rising, falling = edges[z, piece]

            @pl.when(has_up)
            def _():
                falling.wait_recv()

            @pl.when(has_down)
            def _():
                rising.wait_recv()

    first = [
        start(vectors.at[:, half], relay.at[:, half], at[route])
        for half, route in zip(halves, z_routes)
    ]
    own = spread(0, vectors)
    local = [
        pltpu.make_async_copy(vectors, middle(0, 0), local_sems.at[0]),
        pltpu.make_async_copy(blocks, held, local_sems.at[1]),
    ]
    for copy in local:
        copy.start()
    second = []
    for n, (copy, route) in enumerate(zip(first, z_routes)):
        copy.wait_recv()
        second.append(start(relay.at[:, halves[n]], middle(1, 0, n * cut, cut), at[route]))
    own_far = forward(0, *own)
    for copy in second:
        copy.wait_recv()
    other = spread(1, middle(1, 0))
    for copy in own_far:
        copy.wait_recv()
    halo(0, 3, middle(0, 3))
    other_far = forward(1, *other)
    for copy in other_far:
        copy.wait_recv()
    halo(1, 3, middle(1, 3))
    for copy in local:
        copy.wait()

    chunk = width // CHUNKS
    units = [(z, q) for z in (0, 1) for q in range(CHUNKS)]
    index = {unit: n for n, unit in enumerate(units)}
    ways = (("right", "left", 1, 2), ("left", "right", 2, 1))
    far, near, joint, hop, final = {}, {}, {}, {}, {}

    def part(n, piece):
        return partial.at[n, pl.ds(piece * states, states)]

    def multiply(unit):
        z, q = unit
        n = index[unit]
        panel = panels[z]

        def one_row(i, carry):
            row = q * (rows // CHUNKS) + i
            base = row * slots
            total = None
            for first in range(0, slots, 2):
                group = range(first, min(first + 2, slots))
                picked = [panel[relative[base + k]] for k in group]
                weight = [
                    held[row, k] * jnp.full((size, size), live[base + k]).astype(held.dtype)
                    for k in group
                ]
                term = lax.dot_general(
                    jnp.concatenate(picked, axis=1),
                    jnp.concatenate(weight, axis=1),
                    (((1,), (1,)), ((), ())),
                    preferred_element_type=jnp.float32,
                )
                total = term if total is None else total + term
            partial[n, :, pl.ds(pl.multiple_of(i * size, size), size)] = total
            return carry

        lax.fori_loop(0, rows // CHUNKS, one_row, 0)

    def send(unit):
        multiply(unit)
        to, back, _, plain = ways[unit[1] % 2]
        n = index[unit]
        far[unit] = start(part(n, 3), passing.at[n], at[to])
        near[unit] = start(part(n, plain), direct.at[n], at[back])

    def join(unit):
        to, _, piece, _ = ways[unit[1] % 2]
        n = index[unit]
        far[unit].wait_recv()
        passing[n] = part(n, piece)[...] + passing[n]
        joint[unit] = start(passing.at[n], joined.at[n], at[to])

    def finish(unit):
        z, q = unit
        n = index[unit]
        joint[unit].wait_recv()
        near[unit].wait_recv()
        joined[n] = part(n, 0)[...] + joined[n] + direct[n]
        if z == 1:
            hop[q] = start(joined.at[n], hopping.at[q], at[z_routes[q % 2]])

    def pass_on(unit):
        q = unit[1]
        hop[q].wait_recv()
        final[q] = start(hopping.at[q], away.at[q], at[z_routes[q % 2]])

    pairs = [units[i : i + 2] for i in range(0, len(units), 2)]

    def each(step, n):
        for unit in pairs[n]:
            step(unit)

    edges_arrived(0)
    each(send, 0)
    each(send, 1)
    each(join, 0)
    edges_arrived(1)
    each(send, 2)
    each(join, 1)
    each(send, 3)
    each(join, 2)
    each(finish, 0)
    each(join, 3)
    each(finish, 1)
    each(finish, 2)
    each(pass_on, 2)
    each(finish, 3)
    each(pass_on, 3)
    for q in range(CHUNKS):
        final[q].wait_recv()
        out[:, pl.ds(q * chunk, chunk)] = (joined[index[0, q]] + away[q]).astype(out.dtype)

    for copy in started:
        copy.wait_send()
    for rising, falling in edges.values():

        @pl.when(has_up)
        def _():
            rising.wait_send()

        @pl.when(has_down)
        def _():
            falling.wait_send()


def sigma(relative, live, vectors, blocks):
    rows, slots, size, _ = blocks.shape
    states, width = vectors.shape[1], rows * size
    chunk = width // CHUNKS
    copies = 2 + 2 + 2 * 4 + 8 * 2 + 2 * CHUNKS * 3 + CHUNKS * 2
    panel = pltpu.VMEM((rows + 2 * W, 4 * states, size), vectors.dtype)
    all_units = pltpu.VMEM((2 * CHUNKS, states, chunk), jnp.float32)
    half_units = pltpu.VMEM((CHUNKS, states, chunk), jnp.float32)
    return pl.pallas_call(
        sigma_kernel,
        out_shape=jax.ShapeDtypeStruct((states, width), jnp.bfloat16),
        in_specs=[pl.BlockSpec(memory_space=pltpu.SMEM)] * 2
        + [pl.BlockSpec(memory_space=pl.ANY)] * 2,
        out_specs=pl.BlockSpec(memory_space=pltpu.VMEM),
        scratch_shapes=[
            panel,
            panel,
            pltpu.VMEM(blocks.shape, blocks.dtype),
            pltpu.VMEM(vectors.shape, vectors.dtype),
            pltpu.VMEM((2 * CHUNKS, 4 * states, chunk), jnp.float32),
            all_units,
            all_units,
            all_units,
            half_units,
            half_units,
            pltpu.SemaphoreType.DMA((copies,)),
            pltpu.SemaphoreType.DMA((copies,)),
            pltpu.SemaphoreType.DMA((2,)),
        ],
        compiler_params=pltpu.CompilerParams(
            collective_id=0, has_side_effects=True, vmem_limit_bytes=60 * 1024 * 1024
        ),
    )(relative, live, vectors, blocks)


def on_device(vectors, blocks, columns, counts):
    rows, slots, size, _ = blocks.shape
    first_block = lax.axis_index("basis") * rows - W
    relative = (columns - first_block).reshape(-1)
    slot_index = lax.axis_index("state") * slots + jnp.arange(slots, dtype=jnp.int32)
    live = (slot_index[None, :] < counts[:, None]).astype(jnp.float32).reshape(-1)
    by_block = jnp.transpose(vectors.reshape(-1, rows, size), (1, 0, 2))
    return sigma(relative, live, by_block, blocks)


def solution(mesh):
    in_specs = (
        P("state", "basis"),
        P("basis", "state", None, None),
        P("basis", "state"),
        P("basis"),
    )
    out_specs = P("state", "basis")
    return jax.shard_map(
        on_device, mesh=mesh, in_specs=in_specs, out_specs=out_specs, check_vma=False
    )
```

```python
import jax
import jax.numpy as jnp
from jax import lax
from jax.experimental import pallas as pl
from jax.experimental.pallas import tpu as pltpu
from jax.sharding import PartitionSpec as P

W = 36
X, Z_HI, Z_LO = 4, 2, 4
CHUNKS = 8
MESH = pl.DeviceIdType.MESH


def places():
    basis, state = lax.axis_index("basis"), lax.axis_index("state")
    inner = lax.axis_size("basis") // Z_LO
    x, z_hi = lax.div(state, Z_HI), lax.rem(state, Z_HI)
    z_lo, rest = lax.div(basis, inner), lax.rem(basis, inner)
    z = z_hi * Z_LO + z_lo

    def along_x(shift):
        return (basis, lax.rem(x + shift + X, X) * Z_HI + z_hi)

    def along_z(shift):
        moved = lax.rem(z + shift + Z_HI * Z_LO, Z_HI * Z_LO)
        return (lax.rem(moved, Z_LO) * inner + rest, x * Z_HI + lax.div(moved, Z_LO))

    return {
        "right": along_x(1),
        "left": along_x(-1),
        "ahead": along_z(2),
        "behind": along_z(-2),
    }


def greet(partners):
    barrier = pltpu.get_barrier_semaphore()
    for device in partners:
        pl.semaphore_signal(barrier, inc=1, device_id=device, device_id_type=MESH)
    pl.semaphore_wait(barrier, len(partners))


def sender(send_sems, recv_sems):
    used = iter(range(send_sems.shape[0]))

    def make(source, target, device):
        n = next(used)
        return pltpu.make_async_remote_copy(
            src_ref=source,
            dst_ref=target,
            send_sem=send_sems.at[n],
            recv_sem=recv_sems.at[n],
            device_id=device,
            device_id_type=MESH,
        )

    return make


def sigma_kernel(
    relative, live, vectors, blocks, out,
    own_panel, other_panel, held, relay, partial, passing, joined, direct, hopping, away,
    send_sems, recv_sems, local_sems,
):
    at = places()
    basis, state = lax.axis_index("basis"), lax.axis_index("state")
    devices = lax.axis_size("basis")
    up = (lax.rem(basis + 1, devices), state)
    down = (lax.rem(basis + devices - 1, devices), state)
    has_up, has_down = basis < devices - 1, basis > 0
    make = sender(send_sems, recv_sems)
    states = vectors.shape[1]
    rows, slots, size, _ = blocks.shape
    width = rows * size
    cut = states // 2
    halves = (pl.ds(0, cut), pl.ds(cut, cut))
    panels = (own_panel, other_panel)
    z_routes = ("ahead", "behind")

    greet([*at.values(), up, down])
    started, edges = [], {}

    def start(source, target, device):
        copy = make(source, target, device)
        copy.start()
        started.append(copy)
        return copy

    def middle(z, piece, first=0, count=states):
        return panels[z].at[pl.ds(W, rows), pl.ds(piece * states + first, count)]

    def halo(z, piece, source):
        lines = pl.ds(piece * states, states)
        low = panels[z].at[pl.ds(0, W), lines]
        high = panels[z].at[pl.ds(W + rows, W), lines]
        rising = make(source.at[pl.ds(rows - W, W)], low, up)
        falling = make(source.at[pl.ds(0, W)], high, down)

        @pl.when(has_up)
        def _():
            rising.start()

        @pl.when(has_down)
        def _():
            falling.start()

        edges[z, piece] = (rising, falling)

    def spread(z, source):
        to_left = start(source, middle(z, 1), at["left"])
        to_right = start(source, middle(z, 2), at["right"])
        halo(z, 0, source)
        return to_left, to_right

    def forward(z, to_left, to_right):
        to_left.wait_recv()
        far = [start(middle(z, 1, 0, cut), middle(z, 3, 0, cut), at["left"])]
        halo(z, 1, middle(z, 1))
        to_right.wait_recv()
        far.append(start(middle(z, 2, cut, cut), middle(z, 3, cut, cut), at["right"]))
        halo(z, 2, middle(z, 2))
        return far

    def edges_arrived(z):
        for piece in range(4):
            rising, falling = edges[z, piece]

            @pl.when(has_up)
            def _():
                falling.wait_recv()

            @pl.when(has_down)
            def _():
                rising.wait_recv()

    first = [
        start(vectors.at[:, half], relay.at[:, half], at[route])
        for half, route in zip(halves, z_routes)
    ]
    own = spread(0, vectors)
    local = [
        pltpu.make_async_copy(vectors, middle(0, 0), local_sems.at[0]),
        pltpu.make_async_copy(blocks, held, local_sems.at[1]),
    ]
    for copy in local:
        copy.start()
    second = []
    for n, (copy, route) in enumerate(zip(first, z_routes)):
        copy.wait_recv()
        second.append(start(relay.at[:, halves[n]], middle(1, 0, n * cut, cut), at[route]))
    own_far = forward(0, *own)
    for copy in second:
        copy.wait_recv()
    other = spread(1, middle(1, 0))
    for copy in own_far:
        copy.wait_recv()
    halo(0, 3, middle(0, 3))
    other_far = forward(1, *other)
    for copy in other_far:
        copy.wait_recv()
    halo(1, 3, middle(1, 3))
    for copy in local:
        copy.wait()

    chunk = width // CHUNKS
    units = [(z, q) for z in (0, 1) for q in range(CHUNKS)]
    index = {unit: n for n, unit in enumerate(units)}
    ways = (("right", "left", 1, 2), ("left", "right", 2, 1))
    far, near, joint, hop, final = {}, {}, {}, {}, {}

    def part(n, piece):
        return partial.at[n, pl.ds(piece * states, states)]

    def multiply(unit):
        z, q = unit
        n = index[unit]
        panel = panels[z]

        def one_row(i, carry):
            row = q * (rows // CHUNKS) + i
            base = row * slots
            total = None
            for first in range(0, slots, 2):
                group = range(first, min(first + 2, slots))
                picked = [panel[relative[base + k]] for k in group]
                weight = [
                    held[row, k] * jnp.full((size, size), live[base + k]).astype(held.dtype)
                    for k in group
                ]
                term = lax.dot_general(
                    jnp.concatenate(picked, axis=1),
                    jnp.concatenate(weight, axis=1),
                    (((1,), (1,)), ((), ())),
                    preferred_element_type=jnp.float32,
                )
                total = term if total is None else total + term
            partial[n, :, pl.ds(pl.multiple_of(i * size, size), size)] = total
            return carry

        lax.fori_loop(0, rows // CHUNKS, one_row, 0)

    def send(unit):
        to, back, _, plain = ways[unit[1] % 2]
        n = index[unit]
        far[unit] = start(part(n, 3), passing.at[n], at[to])
        near[unit] = start(part(n, plain), direct.at[n], at[back])

    def join(unit):
        to, _, piece, _ = ways[unit[1] % 2]
        n = index[unit]
        far[unit].wait_recv()
        passing[n] = part(n, piece)[...] + passing[n]
        joint[unit] = start(passing.at[n], joined.at[n], at[to])

    def finish(unit):
        z, q = unit
        n = index[unit]
        joint[unit].wait_recv()
        near[unit].wait_recv()
        joined[n] = part(n, 0)[...] + joined[n] + direct[n]
        if z == 1:
            hop[q] = start(joined.at[n], hopping.at[q], at[z_routes[q % 2]])

    def pass_on(unit):
        q = unit[1]
        hop[q].wait_recv()
        final[q] = start(hopping.at[q], away.at[q], at[z_routes[q % 2]])

    pairs = [units[i : i + 2] for i in range(0, len(units), 2)]

    def each(step, n):
        for unit in pairs[n]:
            step(unit)

    def feed(unit):
        multiply(unit)
        send(unit)

    edges_arrived(0)
    each(feed, 0)
    each(feed, 1)
    each(join, 0)
    each(multiply, 2)
    each(multiply, 3)
    each(join, 1)
    edges_arrived(1)
    each(feed, 4)
    each(feed, 5)
    each(join, 4)
    each(feed, 6)
    each(join, 5)
    each(feed, 7)
    each(finish, 4)
    each(join, 6)
    each(finish, 5)
    each(pass_on, 4)
    each(join, 7)
    each(send, 2)
    each(send, 3)
    each(finish, 6)
    each(pass_on, 5)
    each(finish, 7)
    each(pass_on, 6)
    each(join, 2)
    each(join, 3)
    each(finish, 0)
    each(finish, 1)
    each(pass_on, 7)
    each(finish, 2)
    each(finish, 3)
    for q in range(CHUNKS):
        final[q].wait_recv()
        out[:, pl.ds(q * chunk, chunk)] = (joined[index[0, q]] + away[q]).astype(out.dtype)

    for copy in started:
        copy.wait_send()
    for rising, falling in edges.values():

        @pl.when(has_up)
        def _():
            rising.wait_send()

        @pl.when(has_down)
        def _():
            falling.wait_send()


def sigma(relative, live, vectors, blocks):
    rows, slots, size, _ = blocks.shape
    states, width = vectors.shape[1], rows * size
    chunk = width // CHUNKS
    copies = 2 + 2 + 2 * 4 + 8 * 2 + 2 * CHUNKS * 3 + CHUNKS * 2
    panel = pltpu.VMEM((rows + 2 * W, 4 * states, size), vectors.dtype)
    all_units = pltpu.VMEM((2 * CHUNKS, states, chunk), jnp.float32)
    half_units = pltpu.VMEM((CHUNKS, states, chunk), jnp.float32)
    return pl.pallas_call(
        sigma_kernel,
        out_shape=jax.ShapeDtypeStruct((states, width), jnp.bfloat16),
        in_specs=[pl.BlockSpec(memory_space=pltpu.SMEM)] * 2
        + [pl.BlockSpec(memory_space=pl.ANY)] * 2,
        out_specs=pl.BlockSpec(memory_space=pltpu.VMEM),
        scratch_shapes=[
            panel,
            panel,
            pltpu.VMEM(blocks.shape, blocks.dtype),
            pltpu.VMEM(vectors.shape, vectors.dtype),
            pltpu.VMEM((2 * CHUNKS, 4 * states, chunk), jnp.float32),
            all_units,
            all_units,
            all_units,
            half_units,
            half_units,
            pltpu.SemaphoreType.DMA((copies,)),
            pltpu.SemaphoreType.DMA((copies,)),
            pltpu.SemaphoreType.DMA((2,)),
        ],
        compiler_params=pltpu.CompilerParams(
            collective_id=0, has_side_effects=True, vmem_limit_bytes=60 * 1024 * 1024
        ),
    )(relative, live, vectors, blocks)


def on_device(vectors, blocks, columns, counts):
    rows, slots, size, _ = blocks.shape
    first_block = lax.axis_index("basis") * rows - W
    relative = (columns - first_block).reshape(-1)
    slot_index = lax.axis_index("state") * slots + jnp.arange(slots, dtype=jnp.int32)
    live = (slot_index[None, :] < counts[:, None]).astype(jnp.float32).reshape(-1)
    by_block = jnp.transpose(vectors.reshape(-1, rows, size), (1, 0, 2))
    return sigma(relative, live, by_block, blocks)


def solution(mesh):
    in_specs = (
        P("state", "basis"),
        P("basis", "state", None, None),
        P("basis", "state"),
        P("basis"),
    )
    out_specs = P("state", "basis")
    return jax.shard_map(
        on_device, mesh=mesh, in_specs=in_specs, out_specs=out_specs, check_vma=False
    )
```

```python
import jax
import jax.numpy as jnp
from jax import lax
from jax.experimental import pallas as pl
from jax.experimental.pallas import tpu as pltpu
from jax.sharding import PartitionSpec as P

W = 36
X, Z_HI, Z_LO = 4, 2, 4
CHUNKS = 8
MESH = pl.DeviceIdType.MESH


def places():
    basis, state = lax.axis_index("basis"), lax.axis_index("state")
    inner = lax.axis_size("basis") // Z_LO
    x, z_hi = lax.div(state, Z_HI), lax.rem(state, Z_HI)
    z_lo, rest = lax.div(basis, inner), lax.rem(basis, inner)
    z = z_hi * Z_LO + z_lo

    def along_x(shift):
        return (basis, lax.rem(x + shift + X, X) * Z_HI + z_hi)

    def along_z(shift):
        moved = lax.rem(z + shift + Z_HI * Z_LO, Z_HI * Z_LO)
        return (lax.rem(moved, Z_LO) * inner + rest, x * Z_HI + lax.div(moved, Z_LO))

    return {
        "right": along_x(1),
        "left": along_x(-1),
        "ahead": along_z(2),
        "behind": along_z(-2),
    }


def greet(partners):
    barrier = pltpu.get_barrier_semaphore()
    for device in partners:
        pl.semaphore_signal(barrier, inc=1, device_id=device, device_id_type=MESH)
    pl.semaphore_wait(barrier, len(partners))


def sender(send_sems, recv_sems):
    used = iter(range(send_sems.shape[0]))

    def make(source, target, device):
        n = next(used)
        return pltpu.make_async_remote_copy(
            src_ref=source,
            dst_ref=target,
            send_sem=send_sems.at[n],
            recv_sem=recv_sems.at[n],
            device_id=device,
            device_id_type=MESH,
        )

    return make


def sigma_kernel(
    relative, live, vectors, blocks, out,
    own_panel, other_panel, held, relay, partial, passing, joined, direct, hopping, away,
    send_sems, recv_sems, local_sems,
):
    at = places()
    basis, state = lax.axis_index("basis"), lax.axis_index("state")
    devices = lax.axis_size("basis")
    up = (lax.rem(basis + 1, devices), state)
    down = (lax.rem(basis + devices - 1, devices), state)
    has_up, has_down = basis < devices - 1, basis > 0
    make = sender(send_sems, recv_sems)
    states = vectors.shape[1]
    rows, slots, size, _ = blocks.shape
    width = rows * size
    cut = states // 2
    fine = cut // 2
    legs = ((0, "ahead"), (cut, "behind"), (fine, "ahead"), (cut + fine, "behind"))
    panels = (own_panel, other_panel)
    z_routes = ("ahead", "behind")

    greet([*at.values(), up, down])
    started, edges = [], {}

    def start(source, target, device):
        copy = make(source, target, device)
        copy.start()
        started.append(copy)
        return copy

    def middle(z, piece, first=0, count=states):
        return panels[z].at[pl.ds(W, rows), pl.ds(piece * states + first, count)]

    def halo(z, piece, source):
        lines = pl.ds(piece * states, states)
        low = panels[z].at[pl.ds(0, W), lines]
        high = panels[z].at[pl.ds(W + rows, W), lines]
        rising = make(source.at[pl.ds(rows - W, W)], low, up)
        falling = make(source.at[pl.ds(0, W)], high, down)

        @pl.when(has_up)
        def _():
            rising.start()

        @pl.when(has_down)
        def _():
            falling.start()

        edges[z, piece] = (rising, falling)

    def spread(z, source):
        to_left = start(source, middle(z, 1), at["left"])
        to_right = start(source, middle(z, 2), at["right"])
        halo(z, 0, source)
        return to_left, to_right

    def forward(z, to_left, to_right):
        to_left.wait_recv()
        far = [start(middle(z, 1, 0, cut), middle(z, 3, 0, cut), at["left"])]
        halo(z, 1, middle(z, 1))
        to_right.wait_recv()
        far.append(start(middle(z, 2, cut, cut), middle(z, 3, cut, cut), at["right"]))
        halo(z, 2, middle(z, 2))
        return far

    def edges_arrived(z):
        for piece in range(4):
            rising, falling = edges[z, piece]

            @pl.when(has_up)
            def _():
                falling.wait_recv()

            @pl.when(has_down)
            def _():
                rising.wait_recv()

    first = [
        start(vectors.at[:, pl.ds(line, fine)], relay.at[:, pl.ds(line, fine)], at[route])
        for line, route in legs
    ]
    own = spread(0, vectors)
    local = [
        pltpu.make_async_copy(vectors, middle(0, 0), local_sems.at[0]),
        pltpu.make_async_copy(blocks, held, local_sems.at[1]),
    ]
    for copy in local:
        copy.start()
    second = []
    for copy, (line, route) in zip(first, legs):
        copy.wait_recv()
        second.append(
            start(relay.at[:, pl.ds(line, fine)], middle(1, 0, line, fine), at[route])
        )
    own_far = forward(0, *own)
    for copy in second:
        copy.wait_recv()
    other = spread(1, middle(1, 0))
    for copy in own_far:
        copy.wait_recv()
    halo(0, 3, middle(0, 3))
    other_far = forward(1, *other)
    for copy in other_far:
        copy.wait_recv()
    halo(1, 3, middle(1, 3))
    for copy in local:
        copy.wait()

    chunk = width // CHUNKS
    units = [(z, q) for z in (0, 1) for q in range(CHUNKS)]
    index = {unit: n for n, unit in enumerate(units)}
    ways = (("right", "left", 1, 2), ("left", "right", 2, 1))
    far, near, joint, hop, final = {}, {}, {}, {}, {}

    def part(n, piece):
        return partial.at[n, pl.ds(piece * states, states)]

    def multiply(unit):
        z, q = unit
        n = index[unit]
        panel = panels[z]

        def one_row(i, carry):
            row = q * (rows // CHUNKS) + i
            base = row * slots
            total = None
            for first in range(0, slots, 2):
                group = range(first, min(first + 2, slots))
                picked = [panel[relative[base + k]] for k in group]
                weight = [
                    held[row, k] * jnp.full((size, size), live[base + k]).astype(held.dtype)
                    for k in group
                ]
                term = lax.dot_general(
                    jnp.concatenate(picked, axis=1),
                    jnp.concatenate(weight, axis=1),
                    (((1,), (1,)), ((), ())),
                    preferred_element_type=jnp.float32,
                )
                total = term if total is None else total + term
            partial[n, :, pl.ds(pl.multiple_of(i * size, size), size)] = total
            return carry

        lax.fori_loop(0, rows // CHUNKS, one_row, 0)

    def send(unit):
        to, back, _, plain = ways[unit[1] % 2]
        n = index[unit]
        far[unit] = start(part(n, 3), passing.at[n], at[to])
        near[unit] = start(part(n, plain), direct.at[n], at[back])

    def join(unit):
        to, _, piece, _ = ways[unit[1] % 2]
        n = index[unit]
        far[unit].wait_recv()
        passing[n] = part(n, piece)[...] + passing[n]
        joint[unit] = start(passing.at[n], joined.at[n], at[to])

    def finish(unit):
        z, q = unit
        n = index[unit]
        joint[unit].wait_recv()
        near[unit].wait_recv()
        joined[n] = part(n, 0)[...] + joined[n] + direct[n]
        if z == 1:
            hop[q] = start(joined.at[n], hopping.at[q], at[z_routes[q % 2]])

    def pass_on(unit):
        q = unit[1]
        hop[q].wait_recv()
        final[q] = start(hopping.at[q], away.at[q], at[z_routes[q % 2]])

    pairs = [units[i : i + 2] for i in range(0, len(units), 2)]

    def each(step, n):
        for unit in pairs[n]:
            step(unit)

    def feed(unit):
        multiply(unit)
        send(unit)

    edges_arrived(0)
    each(feed, 0)
    each(feed, 1)
    each(join, 0)
    each(multiply, 2)
    each(multiply, 3)
    each(join, 1)
    edges_arrived(1)
    each(feed, 4)
    each(feed, 5)
    each(join, 4)
    each(feed, 6)
    each(join, 5)
    each(feed, 7)
    each(finish, 4)
    each(join, 6)
    each(finish, 5)
    each(pass_on, 4)
    each(join, 7)
    each(send, 2)
    each(send, 3)
    each(finish, 6)
    each(pass_on, 5)
    each(finish, 7)
    each(pass_on, 6)
    each(join, 2)
    each(join, 3)
    each(finish, 0)
    each(finish, 1)
    each(pass_on, 7)
    each(finish, 2)
    each(finish, 3)
    for q in range(CHUNKS):
        final[q].wait_recv()
        out[:, pl.ds(q * chunk, chunk)] = (joined[index[0, q]] + away[q]).astype(out.dtype)

    for copy in started:
        copy.wait_send()
    for rising, falling in edges.values():

        @pl.when(has_up)
        def _():
            rising.wait_send()

        @pl.when(has_down)
        def _():
            falling.wait_send()


def sigma(relative, live, vectors, blocks):
    rows, slots, size, _ = blocks.shape
    states, width = vectors.shape[1], rows * size
    chunk = width // CHUNKS
    copies = 4 + 4 + 2 * 4 + 8 * 2 + 2 * CHUNKS * 3 + CHUNKS * 2
    panel = pltpu.VMEM((rows + 2 * W, 4 * states, size), vectors.dtype)
    all_units = pltpu.VMEM((2 * CHUNKS, states, chunk), jnp.float32)
    half_units = pltpu.VMEM((CHUNKS, states, chunk), jnp.float32)
    return pl.pallas_call(
        sigma_kernel,
        out_shape=jax.ShapeDtypeStruct((states, width), jnp.bfloat16),
        in_specs=[pl.BlockSpec(memory_space=pltpu.SMEM)] * 2
        + [pl.BlockSpec(memory_space=pl.ANY)] * 2,
        out_specs=pl.BlockSpec(memory_space=pltpu.VMEM),
        scratch_shapes=[
            panel,
            panel,
            pltpu.VMEM(blocks.shape, blocks.dtype),
            pltpu.VMEM(vectors.shape, vectors.dtype),
            pltpu.VMEM((2 * CHUNKS, 4 * states, chunk), jnp.float32),
            all_units,
            all_units,
            all_units,
            half_units,
            half_units,
            pltpu.SemaphoreType.DMA((copies,)),
            pltpu.SemaphoreType.DMA((copies,)),
            pltpu.SemaphoreType.DMA((2,)),
        ],
        compiler_params=pltpu.CompilerParams(
            collective_id=0, has_side_effects=True, vmem_limit_bytes=60 * 1024 * 1024
        ),
    )(relative, live, vectors, blocks)


def on_device(vectors, blocks, columns, counts):
    rows, slots, size, _ = blocks.shape
    first_block = lax.axis_index("basis") * rows - W
    relative = (columns - first_block).reshape(-1)
    slot_index = lax.axis_index("state") * slots + jnp.arange(slots, dtype=jnp.int32)
    live = (slot_index[None, :] < counts[:, None]).astype(jnp.float32).reshape(-1)
    by_block = jnp.transpose(vectors.reshape(-1, rows, size), (1, 0, 2))
    return sigma(relative, live, by_block, blocks)


def solution(mesh):
    in_specs = (
        P("state", "basis"),
        P("basis", "state", None, None),
        P("basis", "state"),
        P("basis"),
    )
    out_specs = P("state", "basis")
    return jax.shard_map(
        on_device, mesh=mesh, in_specs=in_specs, out_specs=out_specs, check_vma=False
    )
```
